256 devices in a mesh: gx: 8 (over z), gy: 32 (over y, x, core).
Axes of the slice: x: 4, y: 4, z: 8, core: 2. Of those that a mesh axis runs over, the one named last changes fastest.
Arguments:
- coupling: bfloat16 [8, 256, 1024, 512], P('gx', 'gy'), may hold values from -0.44921875 to 0.44921875
- local_block: bfloat16 [8, 256, 512, 512], P('gx', 'gy'), as said below
- counts: int32 [8, 256], P('gx', 'gy'), may hold values from 1 to 4, as said below
- primal: int32 [8, 256, 512], P('gx', 'gy'), may hold values from 0 to 511
- partner: int32 [3, 8], replicated, may hold values from 0 to 7, as said below
Outputs:
- coarse: float32 [8, 512, 512], P('gx')
The draws below stay inside these ranges and needn't reach their ends.
Inputs may be any that keep to these rules, and one draw needn't show every extreme that they name: Each row of partner is a perfect matching of the 8 columns: partner[r, partner[r, c]] == c and partner[r, c] != c. `counts`: in each subdomain column at least one subdomain has all 4 blocks live. `primal`: any constraint may hold any number of rows. `local_block`: diagonal entries are positive.
All inputs are finite; a program needn't handle non-finite values. Where the reference program divides by a largest or mean magnitude, that divisor is 1e-20 or more.
Results may differ from the reference program's by a relative error of at most 0.00078.
Values sent between devices are 32-bit elements; how exact they have to be, the bound alone decides.
A program may use at most 192 MiB of HBM per device.

```python
import math
import jax
import jax.numpy as jnp
from jax import lax

BLK = 128
RB = 4
NI = 1024
NC = 512
ROUNDS = 3
R = 512
NCOL = 8
SUBS = 256


def draw_local_block(key, part):
    first, second = jax.random.split(key)
    shape = (NCOL, SUBS, R, R)
    off = 0.3 * jax.random.normal(first, shape, jnp.float32)
    lead = jnp.exp(jax.random.uniform(second, shape, jnp.float32, math.log(2.0), math.log(20.0)))
    rows = lax.broadcasted_iota(jnp.int32, shape, 2)
    cols = lax.broadcasted_iota(jnp.int32, shape, 3)
    return jnp.where(rows == cols, lead, off).astype(jnp.bfloat16)


def draw_counts(key, part):
    drawn = jax.random.randint(key, (NCOL, SUBS), 1, RB + 1)
    col = lax.broadcasted_iota(jnp.int32, (NCOL, SUBS), 0)
    sub = lax.broadcasted_iota(jnp.int32, (NCOL, SUBS), 1)
    full = sub == (col * 3 + 1) % SUBS
    return jnp.where(full, RB, drawn).astype(jnp.int32)


def draw_partner(key, part):

    def single(round_key):
        order = jax.random.permutation(round_key, NCOL).astype(jnp.int32)
        place = jnp.argsort(order, stable=True).astype(jnp.int32)
        return order[jnp.bitwise_xor(place, 1)]
    keys = jax.random.split(key, ROUNDS)
    return jax.vmap(single)(keys).astype(jnp.int32)


def set_ends(entries, own_key, least, top_value):
    shape = entries.shape
    spot = [jax.random.randint(jax.random.fold_in(own_key, axis), (), 0, shape[axis]) for axis in range(len(shape))]
    entries = entries.at[tuple(spot)].set(least)
    longest = shape.index(max(shape))
    spot[longest] = (spot[longest] + 1) % shape[longest]
    return entries.at[tuple(spot)].set(top_value)


def level_of(rng, extent, pieces, smallest, top_value):
    gain = 1.0
    for dim, blocks in pieces:
        heights = jax.random.uniform(jax.random.fold_in(jax.random.fold_in(rng, 6), dim), (blocks,), jnp.float32, smallest / len(pieces), top_value / len(pieces))
        gain = gain * jnp.repeat(jnp.exp(heights), extent[dim] // blocks).reshape((-1,) + (1,) * (len(extent) - 1 - dim))
    return gain


def normal_values(rng, shape, width, bound, pieces=(), kind=jnp.bfloat16):
    entries = jax.random.normal(rng, shape, jnp.float32) * width
    if len(pieces) > 0:
        entries = level_of(rng, shape, pieces, -0.22, 0.18) * entries
    return jnp.clip(entries, min=-bound, max=bound).astype(kind)


def setup_inputs(seed: int = 0) -> dict:
    streams_of = jax.random.split(jax.random.key(seed), 6)
    return {
        "coupling": normal_values(streams_of[0], (NCOL, SUBS, NI, R), 0.0766, 0.44921875, ((0, 8), (1, 32))),
        "local_block": draw_local_block(jax.random.fold_in(streams_of[5], 71), 0),
        "counts": draw_counts(jax.random.fold_in(streams_of[5], 71), 0),
        "primal": set_ends(jax.random.randint(streams_of[3], (NCOL, SUBS, R), 0, NC), jax.random.fold_in(streams_of[3], 1), 0, NC - 1).astype(jnp.int32),
        "partner": draw_partner(jax.random.fold_in(streams_of[5], 71), 0),
    }


def contribution(coupling_s, block_s, count_s, prim_s, weight_s):
    rows = jnp.arange(R, dtype=jnp.int32)
    live = (rows < count_s * BLK).astype(jnp.float32)
    gram = jnp.dot(coupling_s.T, coupling_s, preferred_element_type=jnp.float32)
    schur = ((block_s.astype(jnp.float32) - gram) * live[:, None] * live[None, :]).astype(jnp.bfloat16)
    onehot = prim_s[:, None] == jnp.arange(NC, dtype=jnp.int32)[None, :]
    basis = jnp.where(onehot, weight_s[:, None], jnp.zeros((), jnp.float32)).astype(jnp.bfloat16)
    image = jnp.dot(schur, basis, preferred_element_type=jnp.float32).astype(jnp.bfloat16)
    return jnp.dot(basis.T, image, preferred_element_type=jnp.float32)

def reference(coupling, local_block, counts, primal, partner):
    stiff = jnp.diagonal(local_block, axis1=2, axis2=3).astype(jnp.float32)
    total = stiff
    for r in range(ROUNDS):
        total = total + stiff[partner[r]]
    weight = stiff / total

    def column(c):

        def step(acc, j):
            term = contribution(coupling[c, j], local_block[c, j], counts[c, j], primal[c, j], weight[c, j])
            return (acc + term, None)
        acc, _ = lax.scan(step, jnp.zeros((NC, NC), jnp.float32), jnp.arange(SUBS, dtype=jnp.int32))
        return acc
    tiles = lax.map(column, jnp.arange(NCOL, dtype=jnp.int32))
    scale = 1.0 / jnp.sqrt(lax.optimization_barrier(jnp.mean(jnp.abs(tiles), axis=2)) + 1e-06)
    return tiles * scale[:, :, None] * scale[:, None, :]
```

```python
import jax
import jax.numpy as jnp
from jax import lax
from jax.experimental import pallas as pl
from jax.experimental.pallas import tpu as pltpu
from jax.sharding import PartitionSpec as P

BLK = 128
NC = 512
ROUNDS = 3
R = 512
NI = 1024
SUBS = 8
NCOL = 8
SIDE = 4
CHIPS = SIDE * SIDE
CB = 256
CHUNKS = NC // CB
HALF = NC // 2
PIECE = HALF // CHIPS
MESH = pl.DeviceIdType.MESH
F32 = jnp.float32
BF16 = jnp.bfloat16

STEPS = (1, 3, 2)
PLANE = sorted(
    [(dy, dx) for dy in range(SIDE) for dx in range(SIDE) if (dy, dx) != (0, 0)],
    key=lambda o: -(min(o[0], SIDE - o[0]) + min(o[1], SIDE - o[1])),
)
LINE = (4, 3, 5, 2, 6, 1, 7)


def kernel(
    coupling, local_block, counts, primal, partner, out,
    c_v, l_v, s_v, bt, img, stiffs, weight, tile, a_recv, b_recv, full,
    c_sem, l_sem, z_send, z_recv, a_send, a_rsem, b_send, b_rsem, g_send, g_rsem, f_send, f_rsem,
):
    gx = lax.axis_index("gx")
    gy = lax.axis_index("gy")
    core = gy % 2
    x = (gy // 2) % SIDE
    y = gy // (2 * SIDE)
    chip = gy // 2

    def at(dy, dx):
        return ((y + dy) % SIDE) * SIDE + (x + dx) % SIDE

    def on(chip_index, core_index):
        return (gx, chip_index * 2 + core_index)

    sibling = on(chip, 1 - core)
    barrier = pltpu.get_barrier_semaphore()
    for dz in LINE:
        pl.semaphore_signal(barrier, inc=1, device_id=((gx + dz) % NCOL, gy), device_id_type=MESH)
    for dy, dx in PLANE:
        pl.semaphore_signal(barrier, inc=1, device_id=on(at(dy, dx), core), device_id_type=MESH)
    pl.semaphore_signal(barrier, inc=1, device_id=sibling, device_id_type=MESH)

    loads_l = [pltpu.make_async_copy(local_block.at[j], l_v.at[j], l_sem.at[j]) for j in range(SUBS)]
    loads_c = [pltpu.make_async_copy(coupling.at[j], c_v.at[j], c_sem.at[j]) for j in range(SUBS)]
    for load in loads_l:
        load.start()
    for load in loads_c:
        load.start()

    eye = lax.broadcasted_iota(jnp.int32, (BLK, BLK), 0) == lax.broadcasted_iota(
        jnp.int32, (BLK, BLK), 1
    )
    for j in range(SUBS):
        loads_l[j].wait()
        for b in range(R // BLK):
            span = pl.ds(BLK * b, BLK)
            block = l_v[j, span, span].astype(F32)
            stiffs[gx, pl.ds(j, 1), span] = jnp.sum(
                jnp.where(eye, block, 0.0), axis=0, keepdims=True
            )
    pl.semaphore_wait(barrier, len(LINE) + len(PLANE) + 1)
    z_copies = []
    for i, dz in enumerate(LINE):
        z_copies.append(
            pltpu.make_async_remote_copy(
                src_ref=stiffs.at[gx],
                dst_ref=stiffs.at[gx],
                send_sem=z_send.at[i],
                recv_sem=z_recv.at[i],
                device_id=((gx + dz) % NCOL, gy),
                device_id_type=MESH,
            )
        )
        z_copies[-1].start()

    columns = lax.broadcasted_iota(jnp.int32, (1, R), 1)
    for j in range(SUBS):
        loads_c[j].wait()
        c = c_v[j]
        gram = lax.dot_general(c, c, (((0,), (0,)), ((), ())), preferred_element_type=F32)
        count = counts[0, j]
        for b in range(R // BLK):
            span = pl.ds(BLK * b, BLK)
            live = (columns < count * BLK) & (b < count)
            s_v[j, span, :] = jnp.where(
                live, l_v[j, span, :].astype(F32) - gram[BLK * b : BLK * (b + 1)], 0.0
            ).astype(BF16)

    for i, dz in enumerate(LINE):
        there = stiffs.at[(gx + NCOL - dz) % NCOL]
        pltpu.make_async_remote_copy(
            src_ref=there, dst_ref=there, send_sem=z_send.at[i], recv_sem=z_recv.at[i],
            device_id=((gx + dz) % NCOL, gy), device_id_type=MESH,
        ).wait_recv()
    stiff = stiffs[gx]
    total = stiff
    for r in range(ROUNDS):
        total = total + stiffs[partner[r, gx]]
    weight[...] = stiff / total
    constraint = lax.broadcasted_iota(jnp.int32, (NC, R), 0)
    for j in range(SUBS):
        bt[j] = jnp.where(
            constraint == primal[pl.ds(j, 1), :], weight[pl.ds(j, 1), :], 0.0
        ).astype(BF16)

    def images(k):
        for j in range(SUBS):
            img[k, j] = lax.dot_general(
                s_v[j], bt[j, pl.ds(k * CB, CB), :], (((1,), (1,)), ((), ())),
                preferred_element_type=F32,
            ).astype(BF16)

    def tiles(k, first, last, so_far):
        for j in range(first, last):
            term = jnp.dot(bt[j], img[k, j], preferred_element_type=F32)
            so_far = term if so_far is None else so_far + term
        return so_far

    mine = pl.ds(pl.multiple_of(core * HALF, HALF), HALF)
    its = pl.ds(pl.multiple_of((1 - core) * HALF, HALF), HALF)

    def piece(chip_index):
        return pl.ds(pl.multiple_of(core * HALF + chip_index * PIECE, PIECE), PIECE)

    def pair_copy(k):
        return pltpu.make_async_remote_copy(
            src_ref=tile.at[k, its], dst_ref=a_recv.at[k], send_sem=a_send.at[k],
            recv_sem=a_rsem.at[k], device_id=sibling, device_id_type=MESH,
        )

    def scatter_copy(k, i):
        dy, dx = PLANE[i]
        return pltpu.make_async_remote_copy(
            src_ref=tile.at[k, piece(at(dy, dx))], dst_ref=b_recv.at[k, i], send_sem=b_send.at[k, i],
            recv_sem=b_rsem.at[k, i], device_id=on(at(dy, dx), core), device_id_type=MESH,
        )

    def gather_copy(k, i, source):
        dy, dx = PLANE[i]
        return pltpu.make_async_remote_copy(
            src_ref=full.at[k, piece(source)], dst_ref=full.at[k, piece(source)],
            send_sem=g_send.at[k, i], recv_sem=g_rsem.at[k, i],
            device_id=on(at(dy, dx), core), device_id_type=MESH,
        )

    def from_chip(i):
        dy, dx = PLANE[i]
        return at(SIDE - dy, SIDE - dx)

    def forward_copy(k, i, rows):
        return pltpu.make_async_remote_copy(
            src_ref=full.at[k, rows], dst_ref=full.at[k, rows], send_sem=f_send.at[k, i],
            recv_sem=f_rsem.at[k, i], device_id=sibling, device_id_type=MESH,
        )

    def scatter(k):
        pair_copy(k).wait()
        tile[k, mine, :] = tile[k, mine, :] + a_recv[k]
        for i in range(len(PLANE)):
            scatter_copy(k, i).start()

    def reduce_and_gather(k):
        own = tile[k, piece(chip), :]
        for i in range(len(PLANE)):
            scatter_copy(k, i).wait_recv()
            own = own + b_recv[k, i]
        full[k, piece(chip), :] = own
        for i in range(len(PLANE)):
            gather_copy(k, i, chip).start()
        forward_copy(k, len(PLANE), piece(chip)).start()

    near_first = range(len(PLANE) - 1, -1, -1)

    def forward(k):
        for i in near_first:
            gather_copy(k, i, from_chip(i)).wait_recv()
            forward_copy(k, i, piece(from_chip(i))).start()

    images(0)
    tile[0] = tiles(0, 0, SUBS, None)
    pair_copy(0).start()
    images(1)
    part = tiles(1, 0, 6, None)
    scatter(0)
    tile[1] = tiles(1, 6, SUBS, part)
    pair_copy(1).start()
    scatter(1)
    for k in range(CHUNKS):
        reduce_and_gather(k)
    for k in range(CHUNKS):
        forward(k)
    other = 1 - core

    def other_piece(chip_index):
        return pl.ds(pl.multiple_of(other * HALF + chip_index * PIECE, PIECE), PIECE)

    for k in range(CHUNKS):
        for i in near_first:
            forward_copy(k, i, other_piece(from_chip(i))).wait_recv()
        forward_copy(k, len(PLANE), other_piece(chip)).wait_recv()

    size = jnp.sum(jnp.abs(full[0]) + jnp.abs(full[1]), axis=1, keepdims=True)
    scale = 1.0 / jnp.sqrt(size / NC + 1e-06)
    across = [
        jnp.sum(jnp.where(eye, scale[BLK * b : BLK * (b + 1)], 0.0), axis=0, keepdims=True)
        for b in range(NC // BLK)
    ]
    across = jnp.concatenate(across, axis=1)
    for k in range(CHUNKS):
        out[:, pl.ds(k * CB, CB)] = full[k] * scale * across[:, k * CB : (k + 1) * CB]

    for copy in z_copies:
        copy.wait_send()
    for k in range(CHUNKS):
        for i in range(len(PLANE)):
            scatter_copy(k, i).wait_send()
            gather_copy(k, i, chip).wait_send()
            forward_copy(k, i, piece(from_chip(i))).wait_send()
        forward_copy(k, len(PLANE), piece(chip)).wait_send()


def per_device(coupling, local_block, counts, primal, partner):
    dma = pltpu.SemaphoreType.DMA
    peers = len(PLANE)
    result = pl.pallas_call(
        kernel,
        name="coarse",
        out_shape=jax.ShapeDtypeStruct((NC, NC), F32),
        in_specs=[
            pl.BlockSpec(memory_space=pltpu.HBM),
            pl.BlockSpec(memory_space=pltpu.HBM),
            pl.BlockSpec(memory_space=pltpu.SMEM),
            pl.BlockSpec(memory_space=pltpu.VMEM),
            pl.BlockSpec(memory_space=pltpu.SMEM),
        ],
        out_specs=pl.BlockSpec(memory_space=pltpu.VMEM),
        scratch_shapes=[
            pltpu.VMEM((SUBS, NI, R), BF16),
            pltpu.VMEM((SUBS, R, R), BF16),
            pltpu.VMEM((SUBS, R, R), BF16),
            pltpu.VMEM((SUBS, NC, R), BF16),
            pltpu.VMEM((CHUNKS, SUBS, R, CB), BF16),
            pltpu.VMEM((NCOL, SUBS, R), F32),
            pltpu.VMEM((SUBS, R), F32),
            pltpu.VMEM((CHUNKS, NC, CB), F32),
            pltpu.VMEM((CHUNKS, HALF, CB), F32),
            pltpu.VMEM((CHUNKS, peers, PIECE, CB), F32),
            pltpu.VMEM((CHUNKS, NC, CB), F32),
            dma((SUBS,)),
            dma((SUBS,)),
            dma((len(LINE),)),
            dma((len(LINE),)),
            dma((CHUNKS,)),
            dma((CHUNKS,)),
            dma((CHUNKS, peers)),
            dma((CHUNKS, peers)),
            dma((CHUNKS, peers)),
            dma((CHUNKS, peers)),
            dma((CHUNKS, peers + 1)),
            dma((CHUNKS, peers + 1)),
        ],
        compiler_params=pltpu.CompilerParams(
            collective_id=0, has_side_effects=True, vmem_limit_bytes=52 << 20
        ),
    )(coupling[0], local_block[0], counts, primal[0], partner)
    return result[None]


def solution(mesh):
    placed = (
        P("gx", "gy", None, None),
        P("gx", "gy", None, None),
        P("gx", "gy"),
        P("gx", "gy", None),
        P(),
    )
    return jax.shard_map(
        per_device, mesh=mesh, in_specs=placed, out_specs=P("gx", None, None), check_vma=False
    )
```

```python
import jax
import jax.numpy as jnp
from jax import lax
from jax.experimental import pallas as pl
from jax.experimental.pallas import tpu as pltpu
from jax.sharding import PartitionSpec as P

BLK = 128
NC = 512
ROUNDS = 3
R = 512
NI = 1024
SUBS = 8
NCOL = 8
SIDE = 4
CHIPS = SIDE * SIDE
CB = 256
CHUNKS = NC // CB
HALF = NC // 2
PIECE = HALF // CHIPS
MESH = pl.DeviceIdType.MESH
F32 = jnp.float32
BF16 = jnp.bfloat16

STEPS = (1, 3, 2)
PLANE = sorted(
    [(dy, dx) for dy in range(SIDE) for dx in range(SIDE) if (dy, dx) != (0, 0)],
    key=lambda o: -(min(o[0], SIDE - o[0]) + min(o[1], SIDE - o[1])),
)
LINE = (4, 3, 5, 2, 6, 1, 7)


def kernel(
    coupling, local_block, counts, primal, partner, out,
    c_v, l_v, d_v, p_v, count_s, partner_s, s_v, bt, img, stiffs, weight, tile, a_recv, b_recv, full,
    c_sem, l_sem, d_sem, o_sem, z_send, z_recv, a_send, a_rsem, b_send, b_rsem, g_send, g_rsem, f_send, f_rsem,
):
    gx = lax.axis_index("gx")
    gy = lax.axis_index("gy")
    core = gy % 2
    x = (gy // 2) % SIDE
    y = gy // (2 * SIDE)
    chip = gy // 2

    def at(dy, dx):
        return ((y + dy) % SIDE) * SIDE + (x + dx) % SIDE

    def on(chip_index, core_index):
        return (gx, chip_index * 2 + core_index)

    def loads(j):
        return (
            pltpu.make_async_copy(coupling.at[j], c_v.at[j], c_sem.at[j]),
            pltpu.make_async_copy(local_block.at[j], l_v.at[j], l_sem.at[j]),
        )

    def spans(b):
        return pl.ds(BLK * b, BLK)

    diagonal = [
        pltpu.make_async_copy(
            local_block.at[:, spans(b), spans(b)], d_v.at[b], d_sem.at[b]
        )
        for b in range(R // BLK)
    ]
    small = [
        pltpu.make_async_copy(primal, p_v, o_sem.at[0]),
        pltpu.make_async_copy(counts, count_s, o_sem.at[1]),
        pltpu.make_async_copy(partner, partner_s, o_sem.at[2]),
    ]
    for load in diagonal + small:
        load.start()
    sibling = on(chip, 1 - core)
    barrier = pltpu.get_barrier_semaphore()
    for dz in LINE:
        pl.semaphore_signal(barrier, inc=1, device_id=((gx + dz) % NCOL, gy), device_id_type=MESH)
    for dy, dx in PLANE:
        pl.semaphore_signal(barrier, inc=1, device_id=on(at(dy, dx), core), device_id_type=MESH)
    pl.semaphore_signal(barrier, inc=1, device_id=sibling, device_id_type=MESH)

    for j in range(SUBS):
        for load in loads(j):
            load.start()

    eye = lax.broadcasted_iota(jnp.int32, (BLK, BLK), 0) == lax.broadcasted_iota(
        jnp.int32, (BLK, BLK), 1
    )
    for load in diagonal + small:
        load.wait()
    for b in range(R // BLK):
        for j in range(SUBS):
            stiffs[gx, pl.ds(j, 1), spans(b)] = jnp.sum(
                jnp.where(eye, d_v[b, j].astype(F32), 0.0), axis=0, keepdims=True
            )

    pl.semaphore_wait(barrier, len(LINE) + len(PLANE) + 1)
    z_copies = []
    for i, dz in enumerate(LINE):
        z_copies.append(
            pltpu.make_async_remote_copy(
                src_ref=stiffs.at[gx],
                dst_ref=stiffs.at[gx],
                send_sem=z_send.at[i],
                recv_sem=z_recv.at[i],
                device_id=((gx + dz) % NCOL, gy),
                device_id_type=MESH,
            )
        )
        z_copies[-1].start()

    columns = lax.broadcasted_iota(jnp.int32, (1, R), 1)

    def over_rows(a, b):
        return lax.dot_general(a, b, (((0,), (0,)), ((), ())), preferred_element_type=F32)

    def schur(first, last):
        for j in range(first, last):
            for load in loads(j):
                load.wait()
        for j in range(first, last):
            low, high = c_v[j, :, pl.ds(0, R // 2)], c_v[j, :, pl.ds(R // 2, R // 2)]
            corner = over_rows(low, high)
            upper = jnp.concatenate([over_rows(low, low), corner], axis=1)
            lower = jnp.concatenate([corner.T, over_rows(high, high)], axis=1)
            count = count_s[0, j]
            for b in range(R // BLK):
                live = (columns < count * BLK) & (b < count)
                at_row = BLK * b % (R // 2)
                gram = (upper if 2 * b < R // BLK else lower)[at_row : at_row + BLK]
                s_v[j, spans(b), :] = jnp.where(
                    live, l_v[j, spans(b), :].astype(F32) - gram, 0.0
                ).astype(BF16)

    schur(0, 1)
    schur(1, 3)
    schur(3, SUBS)

    for i, dz in enumerate(LINE):
        there = stiffs.at[(gx + NCOL - dz) % NCOL]
        pltpu.make_async_remote_copy(
            src_ref=there, dst_ref=there, send_sem=z_send.at[i], recv_sem=z_recv.at[i],
            device_id=((gx + dz) % NCOL, gy), device_id_type=MESH,
        ).wait_recv()
    stiff = stiffs[gx]
    total = stiff
    for r in range(ROUNDS):
        total = total + stiffs[partner_s[r, gx]]
    weight[...] = stiff / total
    constraint = lax.broadcasted_iota(jnp.int32, (NC, R), 0)
    for j in range(SUBS):
        bt[j] = jnp.where(
            constraint == p_v[pl.ds(j, 1), :], weight[pl.ds(j, 1), :], 0.0
        ).astype(BF16)

    def images(k):
        for j in range(SUBS):
            img[k, j] = lax.dot_general(
                s_v[j], bt[j, pl.ds(k * CB, CB), :], (((1,), (1,)), ((), ())),
                preferred_element_type=F32,
            ).astype(BF16)

    def half_tile(k, rows):
        so_far = None
        for j in range(SUBS):
            term = jnp.dot(bt[j, rows, :], img[k, j], preferred_element_type=F32)
            so_far = term if so_far is None else so_far + term
        tile[k, rows, :] = so_far

    mine = pl.ds(pl.multiple_of(core * HALF, HALF), HALF)
    its = pl.ds(pl.multiple_of((1 - core) * HALF, HALF), HALF)

    def piece(chip_index):
        return pl.ds(pl.multiple_of(core * HALF + chip_index * PIECE, PIECE), PIECE)

    def pair_copy(k):
        return pltpu.make_async_remote_copy(
            src_ref=tile.at[k, its], dst_ref=a_recv.at[k], send_sem=a_send.at[k],
            recv_sem=a_rsem.at[k], device_id=sibling, device_id_type=MESH,
        )

    def scatter_copy(k, i):
        dy, dx = PLANE[i]
        return pltpu.make_async_remote_copy(
            src_ref=tile.at[k, piece(at(dy, dx))], dst_ref=b_recv.at[k, i], send_sem=b_send.at[k, i],
            recv_sem=b_rsem.at[k, i], device_id=on(at(dy, dx), core), device_id_type=MESH,
        )

    def gather_copy(k, i, source):
        dy, dx = PLANE[i]
        return pltpu.make_async_remote_copy(
            src_ref=full.at[k, piece(source)], dst_ref=full.at[k, piece(source)],
            send_sem=g_send.at[k, i], recv_sem=g_rsem.at[k, i],
            device_id=on(at(dy, dx), core), device_id_type=MESH,
        )

    def from_chip(i):
        dy, dx = PLANE[i]
        return at(SIDE - dy, SIDE - dx)

    def forward_copy(k, i, rows):
        return pltpu.make_async_remote_copy(
            src_ref=full.at[k, rows], dst_ref=full.at[k, rows], send_sem=f_send.at[k, i],
            recv_sem=f_rsem.at[k, i], device_id=sibling, device_id_type=MESH,
        )

    def scatter(k):
        pair_copy(k).wait()
        tile[k, mine, :] = tile[k, mine, :] + a_recv[k]
        for i in range(len(PLANE)):
            scatter_copy(k, i).start()

    def reduce_and_gather(k):
        own = tile[k, piece(chip), :]
        for i in range(len(PLANE)):
            scatter_copy(k, i).wait_recv()
            own = own + b_recv[k, i]
        full[k, piece(chip), :] = own
        for i in range(len(PLANE)):
            gather_copy(k, i, chip).start()
        forward_copy(k, len(PLANE), piece(chip)).start()

    near_first = range(len(PLANE) - 1, -1, -1)

    def forward(k):
        for i in near_first:
            gather_copy(k, i, from_chip(i)).wait_recv()
            forward_copy(k, i, piece(from_chip(i))).start()

    images(0)
    half_tile(0, its)
    pair_copy(0).start()
    half_tile(0, mine)
    images(1)
    scatter(0)
    half_tile(1, its)
    pair_copy(1).start()
    half_tile(1, mine)
    scatter(1)
    for k in range(CHUNKS):
        reduce_and_gather(k)
    for k in range(CHUNKS):
        forward(k)
    other = 1 - core

    def other_piece(chip_index):
        return pl.ds(pl.multiple_of(other * HALF + chip_index * PIECE, PIECE), PIECE)

    size = 0.0
    for k in range(CHUNKS):
        for i in near_first:
            forward_copy(k, i, other_piece(from_chip(i))).wait_recv()
        forward_copy(k, len(PLANE), other_piece(chip)).wait_recv()
        size = size + jnp.sum(jnp.abs(full[k]), axis=1, keepdims=True)

    scale = 1.0 / jnp.sqrt(size / NC + 1e-06)
    across = [
        jnp.sum(jnp.where(eye, scale[BLK * b : BLK * (b + 1)], 0.0), axis=0, keepdims=True)
        for b in range(NC // BLK)
    ]
    across = jnp.concatenate(across, axis=1)
    for k in range(CHUNKS):
        out[:, pl.ds(k * CB, CB)] = full[k] * scale * across[:, k * CB : (k + 1) * CB]

    for copy in z_copies:
        copy.wait_send()
    for k in range(CHUNKS):
        for i in range(len(PLANE)):
            scatter_copy(k, i).wait_send()
            gather_copy(k, i, chip).wait_send()
            forward_copy(k, i, piece(from_chip(i))).wait_send()
        forward_copy(k, len(PLANE), piece(chip)).wait_send()


def in_hbm(x):
    return pltpu.with_memory_space_constraint(x, pltpu.HBM)


def per_device(coupling, local_block, counts, primal, partner):
    dma = pltpu.SemaphoreType.DMA
    peers = len(PLANE)
    result = pl.pallas_call(
        kernel,
        name="coarse",
        out_shape=jax.ShapeDtypeStruct((NC, NC), F32),
        in_specs=[
            pl.BlockSpec(memory_space=pltpu.HBM),
            pl.BlockSpec(memory_space=pltpu.HBM),
            pl.BlockSpec(memory_space=pltpu.HBM),
            pl.BlockSpec(memory_space=pltpu.HBM),
            pl.BlockSpec(memory_space=pltpu.HBM),
        ],
        out_specs=pl.BlockSpec(memory_space=pltpu.VMEM),
        scratch_shapes=[
            pltpu.VMEM((SUBS, NI, R), BF16),
            pltpu.VMEM((SUBS, R, R), BF16),
            pltpu.VMEM((R // BLK, SUBS, BLK, BLK), BF16),
            pltpu.VMEM((SUBS, R), jnp.int32),
            pltpu.SMEM((1, SUBS), jnp.int32),
            pltpu.SMEM((ROUNDS, NCOL), jnp.int32),
            pltpu.VMEM((SUBS, R, R), BF16),
            pltpu.VMEM((SUBS, NC, R), BF16),
            pltpu.VMEM((CHUNKS, SUBS, R, CB), BF16),
            pltpu.VMEM((NCOL, SUBS, R), F32),
            pltpu.VMEM((SUBS, R), F32),
            pltpu.VMEM((CHUNKS, NC, CB), F32),
            pltpu.VMEM((CHUNKS, HALF, CB), F32),
            pltpu.VMEM((CHUNKS, peers, PIECE, CB), F32),
            pltpu.VMEM((CHUNKS, NC, CB), F32),
            dma((SUBS,)),
            dma((SUBS,)),
            dma((R // BLK,)),
            dma((3,)),
            dma((len(LINE),)),
            dma((len(LINE),)),
            dma((CHUNKS,)),
            dma((CHUNKS,)),
            dma((CHUNKS, peers)),
            dma((CHUNKS, peers)),
            dma((CHUNKS, peers)),
            dma((CHUNKS, peers)),
            dma((CHUNKS, peers + 1)),
            dma((CHUNKS, peers + 1)),
        ],
        compiler_params=pltpu.CompilerParams(
            collective_id=0, has_side_effects=True, vmem_limit_bytes=52 << 20
        ),
    )(coupling[0], local_block[0], *(in_hbm(x) for x in (counts, primal[0], partner)))
    return result[None]


def solution(mesh):
    placed = (
        P("gx", "gy", None, None),
        P("gx", "gy", None, None),
        P("gx", "gy"),
        P("gx", "gy", None),
        P(),
    )
    return jax.shard_map(
        per_device, mesh=mesh, in_specs=placed, out_specs=P("gx", None, None), check_vma=False
    )
```

```python
import jax
import jax.numpy as jnp
from jax import lax
from jax.experimental import pallas as pl
from jax.experimental.pallas import tpu as pltpu
from jax.sharding import PartitionSpec as P

BLK = 128
NC = 512
ROUNDS = 3
R = 512
NI = 1024
SUBS = 8
NCOL = 8
SIDE = 4
CHIPS = SIDE * SIDE
CB = 256
CHUNKS = NC // CB
HALF = NC // 2
PIECE = HALF // CHIPS
MESH = pl.DeviceIdType.MESH
F32 = jnp.float32
BF16 = jnp.bfloat16

STEPS = (1, 3, 2)
PLANE = sorted(
    [(dy, dx) for dy in range(SIDE) for dx in range(SIDE) if (dy, dx) != (0, 0)],
    key=lambda o: -(min(o[0], SIDE - o[0]) + min(o[1], SIDE - o[1])),
)
LINE = (4, 3, 5, 2, 6, 1, 7)


def kernel(
    coupling, local_block, counts, primal, partner, out,
    c_v, l_v, d_v, p_v, count_s, partner_s, s_v, bt, img, stiffs, weight, tile, a_recv, b_recv, full, sums,
    c_sem, l_sem, d_sem, o_sem, z_send, z_recv, a_send, a_rsem, b_send, b_rsem, g_send, g_rsem, f_send, f_rsem,
):
    gx = lax.axis_index("gx")
    gy = lax.axis_index("gy")
    core = gy % 2
    x = (gy // 2) % SIDE
    y = gy // (2 * SIDE)
    chip = gy // 2

    def at(dy, dx):
        return ((y + dy) % SIDE) * SIDE + (x + dx) % SIDE

    def on(chip_index, core_index):
        return (gx, chip_index * 2 + core_index)

    def loads(j):
        return (
            pltpu.make_async_copy(coupling.at[j], c_v.at[j], c_sem.at[j]),
            pltpu.make_async_copy(local_block.at[j], l_v.at[j], l_sem.at[j]),
        )

    def spans(b):
        return pl.ds(BLK * b, BLK)

    diagonal = [
        pltpu.make_async_copy(
            local_block.at[:, spans(b), spans(b)], d_v.at[b], d_sem.at[b]
        )
        for b in range(R // BLK)
    ]
    small = [
        pltpu.make_async_copy(primal, p_v, o_sem.at[0]),
        pltpu.make_async_copy(counts, count_s, o_sem.at[1]),
        pltpu.make_async_copy(partner, partner_s, o_sem.at[2]),
    ]
    for load in diagonal + small:
        load.start()
    sibling = on(chip, 1 - core)
    barrier = pltpu.get_barrier_semaphore()
    for dz in LINE:
        pl.semaphore_signal(barrier, inc=1, device_id=((gx + dz) % NCOL, gy), device_id_type=MESH)
    for dy, dx in PLANE:
        pl.semaphore_signal(barrier, inc=1, device_id=on(at(dy, dx), core), device_id_type=MESH)
    pl.semaphore_signal(barrier, inc=1, device_id=sibling, device_id_type=MESH)

    for j in range(SUBS):
        for load in loads(j):
            load.start()

    eye = lax.broadcasted_iota(jnp.int32, (BLK, BLK), 0) == lax.broadcasted_iota(
        jnp.int32, (BLK, BLK), 1
    )
    for load in diagonal + small:
        load.wait()
    for b in range(R // BLK):
        for j in range(SUBS):
            stiffs[gx, pl.ds(j, 1), spans(b)] = jnp.sum(
                jnp.where(eye, d_v[b, j].astype(F32), 0.0), axis=0, keepdims=True
            )

    pl.semaphore_wait(barrier, len(LINE) + len(PLANE) + 1)
    z_copies = []
    for i, dz in enumerate(LINE):
        z_copies.append(
            pltpu.make_async_remote_copy(
                src_ref=stiffs.at[gx],
                dst_ref=stiffs.at[gx],
                send_sem=z_send.at[i],
                recv_sem=z_recv.at[i],
                device_id=((gx + dz) % NCOL, gy),
                device_id_type=MESH,
            )
        )
        z_copies[-1].start()

    columns = lax.broadcasted_iota(jnp.int32, (1, R), 1)

    def over_rows(a, b):
        return lax.dot_general(a, b, (((0,), (0,)), ((), ())), preferred_element_type=F32)

    def schur(first, last):
        for j in range(first, last):
            for load in loads(j):
                load.wait()
        for j in range(first, last):
            low, high = c_v[j, :, pl.ds(0, R // 2)], c_v[j, :, pl.ds(R // 2, R // 2)]
            corner = over_rows(low, high)
            upper = jnp.concatenate([over_rows(low, low), corner], axis=1)
            lower = jnp.concatenate([corner.T, over_rows(high, high)], axis=1)
            count = count_s[0, j]
            for b in range(R // BLK):
                live = (columns < count * BLK) & (b < count)
                at_row = BLK * b % (R // 2)
                gram = (upper if 2 * b < R // BLK else lower)[at_row : at_row + BLK]
                s_v[j, spans(b), :] = jnp.where(
                    live, l_v[j, spans(b), :].astype(F32) - gram, 0.0
                ).astype(BF16)

    schur(0, 1)
    schur(1, 3)
    schur(3, 5)
    schur(5, SUBS)

    for i, dz in enumerate(LINE):
        there = stiffs.at[(gx + NCOL - dz) % NCOL]
        pltpu.make_async_remote_copy(
            src_ref=there, dst_ref=there, send_sem=z_send.at[i], recv_sem=z_recv.at[i],
            device_id=((gx + dz) % NCOL, gy), device_id_type=MESH,
        ).wait_recv()
    stiff = stiffs[gx]
    total = stiff
    for r in range(ROUNDS):
        total = total + stiffs[partner_s[r, gx]]
    weight[...] = stiff / total
    constraint = lax.broadcasted_iota(jnp.int32, (NC, R), 0)
    for j in range(SUBS):
        bt[j] = jnp.where(
            constraint == p_v[pl.ds(j, 1), :], weight[pl.ds(j, 1), :], 0.0
        ).astype(BF16)

    def images(k):
        for j in range(SUBS):
            img[k, j] = lax.dot_general(
                s_v[j], bt[j, pl.ds(k * CB, CB), :], (((1,), (1,)), ((), ())),
                preferred_element_type=F32,
            ).astype(BF16)

    def half_tile(k, rows):
        so_far = None
        for j in range(SUBS):
            term = jnp.dot(bt[j, rows, :], img[k, j], preferred_element_type=F32)
            so_far = term if so_far is None else so_far + term
        tile[k, rows, :] = so_far

    mine = pl.ds(pl.multiple_of(core * HALF, HALF), HALF)
    its = pl.ds(pl.multiple_of((1 - core) * HALF, HALF), HALF)

    def piece(chip_index):
        return pl.ds(pl.multiple_of(core * HALF + chip_index * PIECE, PIECE), PIECE)

    def pair_copy(k):
        return pltpu.make_async_remote_copy(
            src_ref=tile.at[k, its], dst_ref=a_recv.at[k], send_sem=a_send.at[k],
            recv_sem=a_rsem.at[k], device_id=sibling, device_id_type=MESH,
        )

    def scatter_copy(k, i):
        dy, dx = PLANE[i]
        return pltpu.make_async_remote_copy(
            src_ref=tile.at[k, piece(at(dy, dx))], dst_ref=b_recv.at[k, i], send_sem=b_send.at[k, i],
            recv_sem=b_rsem.at[k, i], device_id=on(at(dy, dx), core), device_id_type=MESH,
        )

    def gather_copy(k, i, source):
        dy, dx = PLANE[i]
        return pltpu.make_async_remote_copy(
            src_ref=full.at[k, piece(source)], dst_ref=full.at[k, piece(source)],
            send_sem=g_send.at[k, i], recv_sem=g_rsem.at[k, i],
            device_id=on(at(dy, dx), core), device_id_type=MESH,
        )

    def from_chip(i):
        dy, dx = PLANE[i]
        return at(SIDE - dy, SIDE - dx)

    def forward_copy(k, i, rows):
        return pltpu.make_async_remote_copy(
            src_ref=full.at[k, rows], dst_ref=full.at[k, rows], send_sem=f_send.at[k, i],
            recv_sem=f_rsem.at[k, i], device_id=sibling, device_id_type=MESH,
        )

    def scatter(k):
        pair_copy(k).wait()
        tile[k, mine, :] = tile[k, mine, :] + a_recv[k]
        for i in range(len(PLANE)):
            scatter_copy(k, i).start()

    def reduce_and_gather(k):
        own = tile[k, piece(chip), :]
        for i in range(len(PLANE)):
            scatter_copy(k, i).wait_recv()
            own = own + b_recv[k, i]
        full[k, piece(chip), :] = own
        for i in range(len(PLANE)):
            gather_copy(k, i, chip).start()
        forward_copy(k, len(PLANE), piece(chip)).start()

    near_first = range(len(PLANE) - 1, -1, -1)

    def forward(k):
        for i in near_first:
            gather_copy(k, i, from_chip(i)).wait_recv()
            forward_copy(k, i, piece(from_chip(i))).start()

    def note(k, rows):
        size = jnp.abs(full[k, rows, pl.ds(0, BLK)]) + jnp.abs(full[k, rows, pl.ds(BLK, BLK)])
        sums[rows, :] = size if k == 0 else sums[rows, :] + size

    other = 1 - core

    def other_piece(chip_index, count=1):
        return pl.ds(pl.multiple_of(other * HALF + chip_index * PIECE, PIECE), count * PIECE)

    images(0)
    half_tile(0, its)
    pair_copy(0).start()
    half_tile(0, mine)
    images(1)
    scatter(0)
    half_tile(1, its)
    pair_copy(1).start()
    half_tile(1, mine)
    scatter(1)
    for k in range(CHUNKS):
        reduce_and_gather(k)
    for k in range(CHUNKS):
        forward(k)
        note(k, mine)
    for k in range(CHUNKS):
        for dy in (0, 1, 3, 2):
            if dy == 0:
                forward_copy(k, len(PLANE), other_piece(chip)).wait_recv()
            for i in near_first:
                if (SIDE - PLANE[i][0]) % SIDE == dy:
                    forward_copy(k, i, other_piece(from_chip(i))).wait_recv()
            note(k, other_piece(((y + dy) % SIDE) * SIDE, SIDE))

    across, down = [], []
    for b in range(NC // BLK):
        size = jnp.sum(sums[spans(b), :].T, axis=0, keepdims=True)
        scale = 1.0 / jnp.sqrt(size / NC + 1e-06)
        across.append(scale)
        down.append(jnp.broadcast_to(scale, (BLK, BLK)).T)
    for k in range(CHUNKS):
        for b in range(NC // BLK):
            for h in range(CB // BLK):
                out[spans(b), pl.ds(k * CB + h * BLK, BLK)] = (
                    full[k, spans(b), pl.ds(h * BLK, BLK)] * down[b] * across[k * (CB // BLK) + h]
                )

    for copy in z_copies:
        copy.wait_send()
    for k in range(CHUNKS):
        for i in range(len(PLANE)):
            scatter_copy(k, i).wait_send()
            gather_copy(k, i, chip).wait_send()
            forward_copy(k, i, piece(from_chip(i))).wait_send()
        forward_copy(k, len(PLANE), piece(chip)).wait_send()


def in_hbm(x):
    return pltpu.with_memory_space_constraint(x, pltpu.HBM)


def per_device(coupling, local_block, counts, primal, partner):
    dma = pltpu.SemaphoreType.DMA
    peers = len(PLANE)
    result = pl.pallas_call(
        kernel,
        name="coarse",
        out_shape=jax.ShapeDtypeStruct((NC, NC), F32),
        in_specs=[
            pl.BlockSpec(memory_space=pltpu.HBM),
            pl.BlockSpec(memory_space=pltpu.HBM),
            pl.BlockSpec(memory_space=pltpu.HBM),
            pl.BlockSpec(memory_space=pltpu.HBM),
            pl.BlockSpec(memory_space=pltpu.HBM),
        ],
        out_specs=pl.BlockSpec(memory_space=pltpu.VMEM),
        scratch_shapes=[
            pltpu.VMEM((SUBS, NI, R), BF16),
            pltpu.VMEM((SUBS, R, R), BF16),
            pltpu.VMEM((R // BLK, SUBS, BLK, BLK), BF16),
            pltpu.VMEM((SUBS, R), jnp.int32),
            pltpu.SMEM((1, SUBS), jnp.int32),
            pltpu.SMEM((ROUNDS, NCOL), jnp.int32),
            pltpu.VMEM((SUBS, R, R), BF16),
            pltpu.VMEM((SUBS, NC, R), BF16),
            pltpu.VMEM((CHUNKS, SUBS, R, CB), BF16),
            pltpu.VMEM((NCOL, SUBS, R), F32),
            pltpu.VMEM((SUBS, R), F32),
            pltpu.VMEM((CHUNKS, NC, CB), F32),
            pltpu.VMEM((CHUNKS, HALF, CB), F32),
            pltpu.VMEM((CHUNKS, peers, PIECE, CB), F32),
            pltpu.VMEM((CHUNKS, NC, CB), F32),
            pltpu.VMEM((NC, BLK), F32),
            dma((SUBS,)),
            dma((SUBS,)),
            dma((R // BLK,)),
            dma((3,)),
            dma((len(LINE),)),
            dma((len(LINE),)),
            dma((CHUNKS,)),
            dma((CHUNKS,)),
            dma((CHUNKS, peers)),
            dma((CHUNKS, peers)),
            dma((CHUNKS, peers)),
            dma((CHUNKS, peers)),
            dma((CHUNKS, peers + 1)),
            dma((CHUNKS, peers + 1)),
        ],
        compiler_params=pltpu.CompilerParams(
            collective_id=0, has_side_effects=True, vmem_limit_bytes=52 << 20
        ),
    )(coupling[0], local_block[0], *(in_hbm(x) for x in (counts, primal[0], partner)))
    return result[None]


def solution(mesh):
    placed = (
        P("gx", "gy", None, None),
        P("gx", "gy", None, None),
        P("gx", "gy"),
        P("gx", "gy", None),
        P(),
    )
    return jax.shard_map(
        per_device, mesh=mesh, in_specs=placed, out_specs=P("gx", None, None), check_vma=False
    )
```

```python
import jax
import jax.numpy as jnp
from jax import lax
from jax.experimental import pallas as pl
from jax.experimental.pallas import tpu as pltpu
from jax.sharding import PartitionSpec as P

BLK = 128
NC = 512
ROUNDS = 3
R = 512
NI = 1024
SUBS = 8
PART = SUBS // 2
NCOL = 8
SIDE = 4
CHIPS = SIDE * SIDE
CB = 256
CHUNKS = NC // CB
HALF = NC // 2
PIECE = HALF // CHIPS
MESH = pl.DeviceIdType.MESH
F32 = jnp.float32
BF16 = jnp.bfloat16

STEPS = (1, 3, 2)
PLANE = sorted(
    [(dy, dx) for dy in range(SIDE) for dx in range(SIDE) if (dy, dx) != (0, 0)],
    key=lambda o: -(min(o[0], SIDE - o[0]) + min(o[1], SIDE - o[1])),
)
LINE = (4, 3, 5, 2, 6, 1, 7)


def kernel(
    coupling, local_block, counts, primal, partner, out,
    c_v, l_v, d_v, p_v, count_s, partner_s, s_v, bt, img, stiffs_a, stiffs_b, weight, tile, a_recv, b_recv, full, sums,
    c_sem, l_sem, d_sem, o_sem, z_send, z_recv, a_send, a_rsem, b_send, b_rsem, g_send, g_rsem, f_send, f_rsem,
):
    gx = lax.axis_index("gx")
    gy = lax.axis_index("gy")
    core = gy % 2
    x = (gy // 2) % SIDE
    y = gy // (2 * SIDE)
    chip = gy // 2

    def at(dy, dx):
        return ((y + dy) % SIDE) * SIDE + (x + dx) % SIDE

    def on(chip_index, core_index):
        return (gx, chip_index * 2 + core_index)

    def loads(j):
        return (
            pltpu.make_async_copy(coupling.at[j], c_v.at[j], c_sem.at[j]),
            pltpu.make_async_copy(local_block.at[j], l_v.at[j], l_sem.at[j]),
        )

    def spans(b):
        return pl.ds(BLK * b, BLK)

    diagonal = [
        pltpu.make_async_copy(
            local_block.at[:, spans(b), spans(b)], d_v.at[b], d_sem.at[b]
        )
        for b in range(R // BLK)
    ]
    small = [
        pltpu.make_async_copy(primal, p_v, o_sem.at[0]),
        pltpu.make_async_copy(counts, count_s, o_sem.at[1]),
        pltpu.make_async_copy(partner, partner_s, o_sem.at[2]),
    ]
    for load in diagonal + small:
        load.start()
    sibling = on(chip, 1 - core)
    barrier = pltpu.get_barrier_semaphore()
    for dz in LINE:
        pl.semaphore_signal(barrier, inc=1, device_id=((gx + dz) % NCOL, gy), device_id_type=MESH)
    for dy, dx in PLANE:
        pl.semaphore_signal(barrier, inc=1, device_id=on(at(dy, dx), core), device_id_type=MESH)
    pl.semaphore_signal(barrier, inc=1, device_id=sibling, device_id_type=MESH)

    for j in range(SUBS):
        for load in loads(j):
            load.start()

    eye = lax.broadcasted_iota(jnp.int32, (BLK, BLK), 0) == lax.broadcasted_iota(
        jnp.int32, (BLK, BLK), 1
    )
    for load in diagonal + small:
        load.wait()
    stiffs = (stiffs_a, stiffs_b)
    for b in range(R // BLK):
        for j in range(SUBS):
            row = 2 * (j % PART) + 2 * b // (R // BLK)
            stiffs[j // PART][gx, pl.ds(row, 1), pl.ds(BLK * b % (R // 2), BLK)] = jnp.sum(
                jnp.where(eye, d_v[b, j].astype(F32), 0.0), axis=0, keepdims=True
            )

    pl.semaphore_wait(barrier, len(LINE) + len(PLANE) + 1)

    def z_copy(h, i, source):
        return pltpu.make_async_remote_copy(
            src_ref=stiffs[h].at[source],
            dst_ref=stiffs[h].at[source],
            send_sem=z_send.at[h, i],
            recv_sem=z_recv.at[h, i],
            device_id=((gx + LINE[i]) % NCOL, gy),
            device_id_type=MESH,
        )

    for h in range(2):
        for i in range(len(LINE)):
            z_copy(h, i, gx).start()

    columns = lax.broadcasted_iota(jnp.int32, (1, R), 1)

    def over_rows(a, b):
        return lax.dot_general(a, b, (((0,), (0,)), ((), ())), preferred_element_type=F32)

    def schur(first, last):
        for j in range(first, last):
            for load in loads(j):
                load.wait()
        for j in range(first, last):
            low, high = c_v[j, :, pl.ds(0, R // 2)], c_v[j, :, pl.ds(R // 2, R // 2)]
            corner = over_rows(low, high)
            upper = jnp.concatenate([over_rows(low, low), corner], axis=1)
            lower = jnp.concatenate([corner.T, over_rows(high, high)], axis=1)
            count = count_s[0, j]
            for b in range(R // BLK):
                live = (columns < count * BLK) & (b < count)
                at_row = BLK * b % (R // 2)
                gram = (upper if 2 * b < R // BLK else lower)[at_row : at_row + BLK]
                s_v[j, spans(b), :] = jnp.where(
                    live, l_v[j, spans(b), :].astype(F32) - gram, 0.0
                ).astype(BF16)

    schur(0, 1)
    schur(1, 3)
    schur(3, 5)
    schur(5, SUBS)

    constraint = lax.broadcasted_iota(jnp.int32, (NC, R), 0)

    def bases(h):
        for i, dz in enumerate(LINE):
            z_copy(h, i, (gx + NCOL - dz) % NCOL).wait_recv()
        stiff = stiffs[h][gx]
        total = stiff
        for r in range(ROUNDS):
            total = total + stiffs[h][partner_s[r, gx]]
        weight[h] = stiff / total
        for q in range(PART):
            row = jnp.concatenate(
                [weight[h, pl.ds(2 * q, 1), :], weight[h, pl.ds(2 * q + 1, 1), :]], axis=1
            )
            j = h * PART + q
            bt[j] = jnp.where(constraint == p_v[pl.ds(j, 1), :], row, 0.0).astype(BF16)

    def images(k, first, last):
        for j in range(first, last):
            img[k, j] = lax.dot_general(
                s_v[j], bt[j, pl.ds(k * CB, CB), :], (((1,), (1,)), ((), ())),
                preferred_element_type=F32,
            ).astype(BF16)

    def half_tile(k, rows):
        so_far = None
        for j in range(SUBS):
            term = jnp.dot(bt[j, rows, :], img[k, j], preferred_element_type=F32)
            so_far = term if so_far is None else so_far + term
        tile[k, rows, :] = so_far

    mine = pl.ds(pl.multiple_of(core * HALF, HALF), HALF)
    its = pl.ds(pl.multiple_of((1 - core) * HALF, HALF), HALF)

    def piece(chip_index):
        return pl.ds(pl.multiple_of(core * HALF + chip_index * PIECE, PIECE), PIECE)

    def pair_copy(k):
        return pltpu.make_async_remote_copy(
            src_ref=tile.at[k, its], dst_ref=a_recv.at[k], send_sem=a_send.at[k],
            recv_sem=a_rsem.at[k], device_id=sibling, device_id_type=MESH,
        )

    def scatter_copy(k, i):
        dy, dx = PLANE[i]
        return pltpu.make_async_remote_copy(
            src_ref=tile.at[k, piece(at(dy, dx))], dst_ref=b_recv.at[k, i], send_sem=b_send.at[k, i],
            recv_sem=b_rsem.at[k, i], device_id=on(at(dy, dx), core), device_id_type=MESH,
        )

    def gather_copy(k, i, source):
        dy, dx = PLANE[i]
        return pltpu.make_async_remote_copy(
            src_ref=full.at[k, piece(source)], dst_ref=full.at[k, piece(source)],
            send_sem=g_send.at[k, i], recv_sem=g_rsem.at[k, i],
            device_id=on(at(dy, dx), core), device_id_type=MESH,
        )

    def from_chip(i):
        dy, dx = PLANE[i]
        return at(SIDE - dy, SIDE - dx)

    def forward_copy(k, i, rows):
        return pltpu.make_async_remote_copy(
            src_ref=full.at[k, rows], dst_ref=full.at[k, rows], send_sem=f_send.at[k, i],
            recv_sem=f_rsem.at[k, i], device_id=sibling, device_id_type=MESH,
        )

    def scatter(k):
        pair_copy(k).wait()
        tile[k, mine, :] = tile[k, mine, :] + a_recv[k]
        for i in range(len(PLANE)):
            scatter_copy(k, i).start()

    def reduce_and_gather(k):
        own = tile[k, piece(chip), :]
        for i in range(len(PLANE)):
            scatter_copy(k, i).wait_recv()
            own = own + b_recv[k, i]
        full[k, piece(chip), :] = own
        for i in range(len(PLANE)):
            gather_copy(k, i, chip).start()
        forward_copy(k, len(PLANE), piece(chip)).start()

    near_first = range(len(PLANE) - 1, -1, -1)

    def forward(k):
        for i in range(len(PLANE)):
            gather_copy(k, i, from_chip(i)).wait_recv()
            forward_copy(k, i, piece(from_chip(i))).start()

    def note(k, rows):
        size = jnp.abs(full[k, rows, pl.ds(0, BLK)]) + jnp.abs(full[k, rows, pl.ds(BLK, BLK)])
        sums[rows, :] = size if k == 0 else sums[rows, :] + size

    other = 1 - core

    def other_piece(chip_index, count=1):
        return pl.ds(pl.multiple_of(other * HALF + chip_index * PIECE, PIECE), count * PIECE)

    bases(0)
    images(0, 0, PART)
    bases(1)
    images(0, PART, SUBS)
    half_tile(0, its)
    pair_copy(0).start()
    half_tile(0, mine)
    images(1, 0, SUBS)
    scatter(0)
    half_tile(1, its)
    pair_copy(1).start()
    half_tile(1, mine)
    scatter(1)
    for k in range(CHUNKS):
        reduce_and_gather(k)
    for k in range(CHUNKS):
        forward(k)
        note(k, mine)
    for k in range(CHUNKS):
        for dy in (0, 1, 3, 2):
            if dy == 0:
                forward_copy(k, len(PLANE), other_piece(chip)).wait_recv()
            for i in near_first:
                if (SIDE - PLANE[i][0]) % SIDE == dy:
                    forward_copy(k, i, other_piece(from_chip(i))).wait_recv()
            note(k, other_piece(((y + dy) % SIDE) * SIDE, SIDE))

    across, down = [], []
    for b in range(NC // BLK):
        size = jnp.sum(sums[spans(b), :].T, axis=0, keepdims=True)
        scale = 1.0 / jnp.sqrt(size / NC + 1e-06)
        across.append(scale)
        down.append(jnp.broadcast_to(scale, (BLK, BLK)).T)
    for k in range(CHUNKS):
        for b in range(NC // BLK):
            for h in range(CB // BLK):
                out[spans(b), pl.ds(k * CB + h * BLK, BLK)] = (
                    full[k, spans(b), pl.ds(h * BLK, BLK)] * down[b] * across[k * (CB // BLK) + h]
                )

    for h in range(2):
        for i in range(len(LINE)):
            z_copy(h, i, gx).wait_send()
    for k in range(CHUNKS):
        for i in range(len(PLANE)):
            scatter_copy(k, i).wait_send()
            gather_copy(k, i, chip).wait_send()
            forward_copy(k, i, piece(from_chip(i))).wait_send()
        forward_copy(k, len(PLANE), piece(chip)).wait_send()


def in_hbm(x):
    return pltpu.with_memory_space_constraint(x, pltpu.HBM)


def per_device(coupling, local_block, counts, primal, partner):
    dma = pltpu.SemaphoreType.DMA
    peers = len(PLANE)
    result = pl.pallas_call(
        kernel,
        name="coarse",
        out_shape=jax.ShapeDtypeStruct((NC, NC), F32),
        in_specs=[
            pl.BlockSpec(memory_space=pltpu.HBM),
            pl.BlockSpec(memory_space=pltpu.HBM),
            pl.BlockSpec(memory_space=pltpu.HBM),
            pl.BlockSpec(memory_space=pltpu.HBM),
            pl.BlockSpec(memory_space=pltpu.HBM),
        ],
        out_specs=pl.BlockSpec(memory_space=pltpu.VMEM),
        scratch_shapes=[
            pltpu.VMEM((SUBS, NI, R), BF16),
            pltpu.VMEM((SUBS, R, R), BF16),
            pltpu.VMEM((R // BLK, SUBS, BLK, BLK), BF16),
            pltpu.VMEM((SUBS, R), jnp.int32),
            pltpu.SMEM((1, SUBS), jnp.int32),
            pltpu.SMEM((ROUNDS, NCOL), jnp.int32),
            pltpu.VMEM((SUBS, R, R), BF16),
            pltpu.VMEM((SUBS, NC, R), BF16),
            pltpu.VMEM((CHUNKS, SUBS, R, CB), BF16),
            pltpu.VMEM((NCOL, 2 * PART, R // 2), F32),
            pltpu.VMEM((NCOL, 2 * PART, R // 2), F32),
            pltpu.VMEM((2, 2 * PART, R // 2), F32),
            pltpu.VMEM((CHUNKS, NC, CB), F32),
            pltpu.VMEM((CHUNKS, HALF, CB), F32),
            pltpu.VMEM((CHUNKS, peers, PIECE, CB), F32),
            pltpu.VMEM((CHUNKS, NC, CB), F32),
            pltpu.VMEM((NC, BLK), F32),
            dma((SUBS,)),
            dma((SUBS,)),
            dma((R // BLK,)),
            dma((3,)),
            dma((2, len(LINE))),
            dma((2, len(LINE))),
            dma((CHUNKS,)),
            dma((CHUNKS,)),
            dma((CHUNKS, peers)),
            dma((CHUNKS, peers)),
            dma((CHUNKS, peers)),
            dma((CHUNKS, peers)),
            dma((CHUNKS, peers + 1)),
            dma((CHUNKS, peers + 1)),
        ],
        compiler_params=pltpu.CompilerParams(
            collective_id=0, has_side_effects=True, vmem_limit_bytes=52 << 20
        ),
    )(coupling[0], local_block[0], *(in_hbm(x) for x in (counts, primal[0], partner)))
    return result[None]


def solution(mesh):
    placed = (
        P("gx", "gy", None, None),
        P("gx", "gy", None, None),
        P("gx", "gy"),
        P("gx", "gy", None),
        P(),
    )
    return jax.shard_map(
        per_device, mesh=mesh, in_specs=placed, out_specs=P("gx", None, None), check_vma=False
    )
```
